256 devices in a mesh: seq: 128 (over y, z, x_hi, core), ch: 2 (over x_lo).
Axes of the slice: x: 4 (x_hi: 2, x_lo: 2; x = x_hi * 2 + x_lo), y: 4, z: 8, core: 2. Of those that a mesh axis runs over, the one named last changes fastest.
Arguments:
- qkv: bfloat16 [3, 8192, 16384], P(None, 'ch', 'seq'), parts along dimension 1, may hold values from -6 to 6
- short_filter: float32 [3, 3, 8192], P(None, None, 'ch'), parts along dimension 2, may hold values from -3 to 3
- decay_rate: float32 [8192, 16], P('ch'), parts along dimension 0, may hold values from 1.5258789e-05 to 0.025
- residue: float32 [8192, 16], P('ch'), parts along dimension 0, may hold values from -2 to 2
- skip: float32 [8192], P('ch'), parts along dimension 0, may hold values from 0.1 to 1.9
Outputs:
- output: bfloat16 [8192, 16384], P('ch', 'seq'), parts along dimension 0
The draws below stay inside these ranges and needn't reach their ends.
There are 2 independent parts, one for each index of `ch`. The reference program is written for one: setup_inputs(seed, part) draws one part's arguments, and reference() takes and returns one part's arrays. A program takes and returns all parts, laid end to end along the dimension named above; each array names one. Nothing has to cross between parts.
All inputs are finite; a program needn't handle non-finite values.
Results may differ from the reference program's by a relative error of at most 0.0057.
Values may be sent and summed in bfloat16 or wider, within the bound.
A program may use at most 256 MiB of HBM per device.

```python
import jax
import jax.numpy as jnp
from jax import lax

C = 4096
MODES = 16
SHORT = 3
TOKENS = 16384


def draw_decay_rate(key, part):
    lowest = jnp.log(1.0 / (4.0 * TOKENS))
    highest = jnp.log(1.0 / 40.0)
    spread = jax.random.uniform(key, (C, MODES), jnp.float32)
    return jnp.exp(lowest + (highest - lowest) * spread).astype(jnp.float32)


def shard_levels(key, extent, split, smallest, high):
    factor_of, own = 1.0, jax.random.fold_in(key, 6)
    for dim, blocks in split:
        steps = jnp.exp(jax.random.uniform(jax.random.fold_in(own, dim), (blocks,), jnp.float32, smallest / len(split), high / len(split)))
        factor_of = factor_of * jnp.repeat(steps, extent[dim] // blocks).reshape([-1 if axis == dim else 1 for axis in range(len(extent))])
    return factor_of


def gaussian(stream_key, extent, deviation, bound, pieces=(), kind=jnp.bfloat16):
    level = shard_levels(stream_key, extent, pieces, -0.22, 0.18) if pieces else 1.0
    result = jax.random.normal(stream_key, extent, jnp.float32) * deviation * level
    return jnp.minimum(jnp.maximum(result, -bound), bound).astype(kind)


def setup_inputs(seed: int = 0, part: int = 0) -> dict:
    keys = jax.random.split(jax.random.key(seed), 6)
    part_splits = jax.random.split(jax.random.fold_in(keys[5], part), 6)
    return {
        "qkv": gaussian(part_splits[0], (3, C, TOKENS), 1.0, 6.0, ((2, 128),)),
        "short_filter": gaussian(part_splits[1], (SHORT, 3, C), 0.6, 3.0, (), jnp.float32),
        "decay_rate": draw_decay_rate(jax.random.fold_in(jax.random.fold_in(keys[5], part), 71), part),
        "residue": gaussian(part_splits[3], (C, MODES), 0.35, 2.0, (), jnp.float32),
        "skip": jnp.clip(1.0 + 0.18 * jax.random.normal(part_splits[4], (C,), jnp.float32), 0.1, 1.9),
    }


def group_conv(packed):
    group_gated, group_rates, group_scales = packed
    length = group_gated.shape[1]
    steps = jnp.arange(length, dtype=jnp.float32)
    impulse = jnp.zeros(group_gated.shape, jnp.float32)
    for index in range(MODES):
        impulse = impulse + group_scales[:, index:index + 1] * jnp.exp(-group_rates[:, index:index + 1] * steps[None, :])
    padded = 2 * length
    spectrum = jnp.fft.rfft(impulse, n=padded) * jnp.fft.rfft(group_gated.astype(jnp.float32), n=padded)
    return jnp.fft.irfft(spectrum, n=padded)[:, :length].astype(jnp.float32)

def reference(qkv, short_filter, decay_rate, residue, skip):
    streams = qkv.astype(jnp.float32)
    length = streams.shape[2]
    feat = short_filter[0][:, :, None] * streams
    for index in range(1, SHORT):
        shifted = jnp.pad(streams, ((0, 0), (0, 0), (index, 0)))[:, :, :length]
        feat = feat + short_filter[index][:, :, None] * shifted
    gated = (feat[1] * feat[2]).astype(jnp.bfloat16)
    scales = residue * jnp.sqrt(-jnp.expm1(-2.0 * decay_rate))
    width = 16
    groups = C // width
    conv = lax.map(group_conv, (gated.reshape(groups, width, length), decay_rate.reshape(groups, width, MODES), scales.reshape(groups, width, MODES)))
    conv = conv.reshape(C, length)
    mixed = (conv + skip[:, None] * gated.astype(jnp.float32)).astype(jnp.bfloat16)
    return (feat[0] * mixed.astype(jnp.float32)).astype(jnp.bfloat16)
```

```python
import functools

import jax
import jax.numpy as jnp
from jax import lax
from jax.experimental import pallas as pl
from jax.experimental.pallas import tpu as pltpu
from jax.sharding import PartitionSpec as P

MODES = 16
SHORT = 3
MESH = pl.DeviceIdType.MESH
LANES = 128
CHUNKS = 8
STEPS = 16
F32 = jnp.float32
BF16 = jnp.bfloat16


def cols(block):
    return pl.ds(pl.multiple_of(block * LANES, LANES), LANES)


def wide(row):
    return jnp.broadcast_to(row, (CHUNKS, LANES))


def rounded(value):
    return value.astype(BF16).astype(F32)


def one_minus_exp(x):
    series = 1.0 - x * (1.0 / 7.0)
    for k in (6, 5, 4, 3, 2):
        series = 1.0 - x * (1.0 / k) * series
    return jnp.where(x < 0.25, x * series, 1.0 - jnp.exp(-x))


def kernel(
    n,
    x_hbm,
    taps_hbm,
    rate_hbm,
    residue_hbm,
    skip_hbm,
    out_ref,
    xv,
    taps,
    rate,
    residue,
    skip,
    decay,
    decay14,
    decay15,
    gated,
    states,
    first,
    feat0,
    halo_out,
    halo_in,
    weights,
    near_taps,
    near,
    ends_out,
    ends_in,
    starts_out,
    starts_in,
    load_sems,
    sems,
    own_sem,
):
    me = lax.axis_index("seq")
    blocks = x_hbm.shape[1] // LANES
    parts = n // blocks
    rows = MODES // parts
    following = lax.rem(me + 1, n)

    small = [(rate_hbm, rate), (taps_hbm, taps), (residue_hbm, residue), (skip_hbm, skip)]
    loads = [
        pltpu.make_async_copy(src, dst, load_sems.at[i]) for i, (src, dst) in enumerate(small)
    ]
    loads.append(pltpu.make_async_copy(x_hbm, xv, load_sems.at[len(small)]))
    for load in loads:
        load.start()

    barrier = pltpu.get_barrier_semaphore()

    def greet(i, carry):
        pl.semaphore_signal(
            barrier, inc=1, device_id={"seq": lax.rem(me + i, n)}, device_id_type=MESH
        )
        return carry

    lax.fori_loop(1, n, greet, 0)

    sub = lax.broadcasted_iota(jnp.int32, (CHUNKS, LANES), 0)
    top = sub == 0
    place = lax.broadcasted_iota(jnp.int32, (LANES, LANES), 0)
    token = lax.broadcasted_iota(jnp.int32, (LANES, LANES), 1)
    spread = jnp.where(
        token == lax.rem(place, CHUNKS) * STEPS + lax.div(place, CHUNKS), 1.0, 0.0
    ).astype(BF16)

    loads[0].wait()

    def prepare(block, carry):
        c = cols(block)
        r = rate[:, c]
        decay[:, c] = jnp.exp(-r)
        decay14[:, c] = jnp.exp(-14.0 * r)
        decay15[:, c] = jnp.exp(-15.0 * r)
        return carry

    lax.fori_loop(0, blocks, prepare, 0)

    for load in loads[1:]:
        load.wait()

    def local(block, carry):
        c = cols(block)
        feats = []
        halo_rows = jnp.zeros((CHUNKS, LANES), F32)
        for stream in range(3):
            moved = lax.dot_general(
                spread,
                xv[stream, c, :],
                (((1,), (1,)), ((), ())),
                preferred_element_type=F32,
            )
            v = [moved[j * CHUNKS : (j + 1) * CHUNKS] for j in range(STEPS)]
            for k in range(2):
                row = 2 * stream + k
                halo_rows = jnp.where(
                    sub == row, pltpu.roll(v[14 + k], row + 1, 0), halo_rows
                )
            back1 = jnp.where(top, 0.0, pltpu.roll(v[15], 1, 0))
            back2 = jnp.where(top, 0.0, pltpu.roll(v[14], 1, 0))
            v = [back2, back1] + v
            f = [wide(taps[k, pl.ds(stream, 1), c]) for k in range(3)]
            feat = [f[0] * v[j + 2] + f[1] * v[j + 1] + f[2] * v[j] for j in range(STEPS)]
            if stream == 0:
                for j in range(STEPS):
                    feat0[j * CHUNKS : (j + 1) * CHUNKS, c] = feat[j]
            else:
                for k in range(2):
                    at = (2 * (stream - 1) + k) * CHUNKS
                    first[at : at + CHUNKS, c] = feat[k]
                feats.append(feat)
        halo_out[:, c] = halo_rows.astype(BF16)
        g = [rounded(feats[0][j] * feats[1][j]) for j in range(STEPS)]
        for j in range(STEPS):
            gated[j * CHUNKS : (j + 1) * CHUNKS, c] = g[j]
        for mode in range(MODES):
            a = wide(decay[pl.ds(mode, 1), c])
            state = g[0]
            for j in range(1, STEPS):
                state = a * state + g[j]
            states[mode * CHUNKS : (mode + 1) * CHUNKS, c] = state
        return carry

    lax.fori_loop(0, blocks, local, 0)

    pl.semaphore_wait(barrier, n - 1)
    halo = pltpu.make_async_remote_copy(
        src_ref=halo_out,
        dst_ref=halo_in,
        send_sem=sems.at[0],
        recv_sem=sems.at[1],
        device_id={"seq": following},
        device_id_type=MESH,
    )
    halo.start()

    def tables(block, carry):
        c = cols(block)
        r = rate[:, c]
        a = decay[:, c]
        w = residue[:, c] * jnp.sqrt(one_minus_exp(2.0 * r))
        direct = skip[pl.ds(block, 1), :]
        for j in range(STEPS):
            near_taps[pl.ds(j, 1), c] = jnp.sum(w, axis=0, keepdims=True) + direct
            direct = 0.0
            w = w * a
            weights[j * MODES : (j + 1) * MODES, c] = w
        return carry

    lax.fori_loop(0, blocks, tables, 0)
    halo.wait()

    late = (CHUNKS - 1 - sub).astype(F32) * float(-STEPS)

    def finish(block, carry):
        c = cols(block)
        h = jnp.where(me == 0, 0.0, halo_in[:, c].astype(F32))

        def add_first(stream):
            f1 = taps[1, pl.ds(stream, 1), c]
            f2 = taps[2, pl.ds(stream, 1), c]
            h2 = h[2 * stream : 2 * stream + 1]
            h1 = h[2 * stream + 1 : 2 * stream + 2]
            return [
                jnp.where(top, wide(f1 * h1 + f2 * h2), 0.0),
                jnp.where(top, wide(f2 * h1), 0.0),
            ]

        more = [add_first(stream) for stream in range(3)]
        change = []
        for k in range(2):
            at = slice(k * CHUNKS, (k + 1) * CHUNKS)
            feat0[at, c] = feat0[at, c] + more[0][k]
            one = first[k * CHUNKS : (k + 1) * CHUNKS, c] + more[1][k]
            two = first[(2 + k) * CHUNKS : (3 + k) * CHUNKS, c] + more[2][k]
            g = rounded(one * two)
            change.append(g - gated[at, c])
            gated[at, c] = g
        sums = []
        for mode in range(MODES):
            at = slice(mode * CHUNKS, (mode + 1) * CHUNKS)
            state = (
                states[at, c]
                + wide(decay15[pl.ds(mode, 1), c]) * change[0]
                + wide(decay14[pl.ds(mode, 1), c]) * change[1]
            )
            states[at, c] = state
            sums.append(
                jnp.sum(
                    state * jnp.exp(wide(rate[pl.ds(mode, 1), c]) * late), axis=0, keepdims=True
                )
            )
        for part in range(parts):
            ends_out[block * parts + part] = jnp.concatenate(
                sums[part * rows : (part + 1) * rows], axis=0
            ).astype(BF16)
        return carry

    lax.fori_loop(0, blocks, finish, 0)

    def exchange(src, dst, send_sem, recv_sem):
        def one(i, carry):
            k = lax.rem(me + i, n)
            pltpu.make_async_remote_copy(
                src_ref=src.at[k],
                dst_ref=dst.at[me],
                send_sem=sems.at[send_sem],
                recv_sem=sems.at[recv_sem],
                device_id={"seq": k},
                device_id_type=MESH,
            ).start()
            return carry

        lax.fori_loop(1, n, one, 0)
        own = pltpu.make_async_copy(src.at[me], dst.at[me], own_sem.at[0])
        own.start()
        others = pltpu.make_async_remote_copy(
            src_ref=src.at[pl.ds(0, n - 1)],
            dst_ref=dst.at[pl.ds(0, n - 1)],
            send_sem=sems.at[send_sem],
            recv_sem=sems.at[recv_sem],
            device_id={"seq": following},
            device_id_type=MESH,
        )
        return own, others

    own, others = exchange(ends_out, ends_in, 2, 3)

    def inside(block, carry):
        c = cols(block)
        g = [gated[j * CHUNKS : (j + 1) * CHUNKS, c] for j in range(STEPS)]
        taps_here = [wide(near_taps[pl.ds(j, 1), c]) for j in range(STEPS)]
        for j in range(STEPS):
            total = taps_here[0] * g[j]
            for i in range(1, j + 1):
                total = total + taps_here[i] * g[j - i]
            near[j * CHUNKS : (j + 1) * CHUNKS, c] = total
        for mode in range(MODES):
            at = slice(mode * CHUNKS, (mode + 1) * CHUNKS)
            step = jnp.exp(wide(rate[pl.ds(mode, 1), c]) * float(-STEPS))
            state = states[at, c]
            for shift in (1, 2, 4):
                state = state + jnp.where(sub < shift, 0.0, step * pltpu.roll(state, shift, 0))
                step = step * step
            states[at, c] = jnp.where(top, 0.0, pltpu.roll(state, 1, 0))
        return carry

    lax.fori_loop(0, blocks, inside, 0)

    mine = lax.div(me, parts)
    part = lax.rem(me, parts)
    r = rate[:, cols(mine)]
    pick = r[0:rows]
    for k in range(1, parts):
        pick = jnp.where(part == k, r[k * rows : (k + 1) * rows], pick)
    across = jnp.exp(pick * float(-LANES))

    own.wait()
    others.wait_recv()

    def carry_on(source, entering):
        starts_out[source] = entering.astype(BF16)
        return across * entering + ends_in[source].astype(F32)

    lax.fori_loop(0, n, carry_on, jnp.zeros((rows, LANES), F32), unroll=8)
    others.wait_send()
    own, others = exchange(starts_out, starts_in, 4, 5)
    own.wait()
    others.wait_recv()

    early = sub.astype(F32) * float(-STEPS)

    def final(block, carry):
        c = cols(block)
        entering = []
        for mode in range(MODES):
            at = slice(mode * CHUNKS, (mode + 1) * CHUNKS)
            if mode % rows == 0:
                group = starts_in[block * parts + mode // rows].astype(F32)
            row = mode % rows
            entering.append(
                states[at, c]
                + wide(group[row : row + 1]) * jnp.exp(wide(rate[pl.ds(mode, 1), c]) * early)
            )
        results = []
        for j in range(STEPS):
            total = near[j * CHUNKS : (j + 1) * CHUNKS, c]
            for mode in range(MODES):
                total = total + wide(weights[pl.ds(j * MODES + mode, 1), c]) * entering[mode]
            results.append(feat0[j * CHUNKS : (j + 1) * CHUNKS, c] * rounded(total))
        turned = jnp.concatenate(results, axis=0).T.astype(BF16)
        out_ref[c, :] = jnp.dot(turned, spread, preferred_element_type=F32).astype(BF16)
        return carry

    lax.fori_loop(0, blocks, final, 0)
    others.wait_send()


def body(n, qkv, short_filter, decay_rate, residue, skip):
    channels, width = qkv.shape[1:]
    blocks = channels // LANES
    parts = n // blocks
    rows = MODES // parts
    anywhere = pl.BlockSpec(memory_space=pl.ANY)
    full = (LANES, channels)
    packet = (n, rows, LANES)
    return pl.pallas_call(
        functools.partial(kernel, n),
        out_shape=jax.ShapeDtypeStruct((channels, width), BF16),
        in_specs=[anywhere] * 5,
        out_specs=pl.BlockSpec(memory_space=pltpu.VMEM),
        scratch_shapes=[
            pltpu.VMEM(qkv.shape, BF16),
            pltpu.VMEM(short_filter.shape, F32),
            pltpu.VMEM((MODES, channels), F32),
            pltpu.VMEM((MODES, channels), F32),
            pltpu.VMEM((blocks, LANES), F32),
            pltpu.VMEM((MODES, channels), F32),
            pltpu.VMEM((MODES, channels), F32),
            pltpu.VMEM((MODES, channels), F32),
            pltpu.VMEM(full, F32),
            pltpu.VMEM(full, F32),
            pltpu.VMEM((4 * CHUNKS, channels), F32),
            pltpu.VMEM(full, F32),
            pltpu.VMEM((CHUNKS, channels), BF16),
            pltpu.VMEM((CHUNKS, channels), BF16),
            pltpu.VMEM((STEPS * MODES, channels), F32),
            pltpu.VMEM((STEPS, channels), F32),
            pltpu.VMEM(full, F32),
            pltpu.VMEM(packet, BF16),
            pltpu.VMEM(packet, BF16),
            pltpu.VMEM(packet, BF16),
            pltpu.VMEM(packet, BF16),
            pltpu.SemaphoreType.DMA((5,)),
            pltpu.SemaphoreType.DMA((6,)),
            pltpu.SemaphoreType.DMA((1,)),
        ],
        compiler_params=pltpu.CompilerParams(collective_id=0, has_side_effects=True),
        name="modal_convolution",
    )(qkv, short_filter, decay_rate.T, residue.T, skip.reshape(blocks, LANES))


def solution(mesh):
    in_specs = (P(None, "ch", "seq"), P(None, None, "ch"), P("ch", None), P("ch", None), P("ch"))
    out_specs = P("ch", "seq")
    return jax.shard_map(
        functools.partial(body, mesh.shape["seq"]),
        mesh=mesh,
        in_specs=in_specs,
        out_specs=out_specs,
        check_vma=False,
    )
```

```python
import functools

import jax
import jax.numpy as jnp
from jax import lax
from jax.experimental import pallas as pl
from jax.experimental.pallas import tpu as pltpu
from jax.sharding import PartitionSpec as P

MODES = 16
SHORT = 3
MESH = pl.DeviceIdType.MESH
LANES = 128
CHUNKS = 8
STEPS = 16
WIDE = 4
DEEP = 8
PIECES = 4
LOCAL_UNROLL = 2
F32 = jnp.float32
BF16 = jnp.bfloat16


def cols(block):
    return pl.ds(pl.multiple_of(block * LANES, LANES), LANES)


def far_first(i, size):
    half = lax.div(i + 1, 2)
    return lax.rem(size + size // 2 + jnp.where(lax.rem(i, 2) == 1, half, -half), size)


def wide(row):
    return jnp.broadcast_to(row, (CHUNKS, LANES))


def rounded(value):
    return value.astype(BF16).astype(F32)


def one_minus_exp(x):
    series = 1.0 - x * (1.0 / 7.0)
    for k in (6, 5, 4, 3, 2):
        series = 1.0 - x * (1.0 / k) * series
    return jnp.where(x < 0.25, x * series, 1.0 - jnp.exp(-x))


def kernel(
    n,
    x_hbm,
    taps_hbm,
    rate_hbm,
    residue_hbm,
    skip_hbm,
    out_hbm,
    out,
    xv,
    taps,
    rate,
    residue,
    skip,
    decay,
    decay14,
    decay15,
    gated,
    states,
    first,
    feat0,
    halo_out,
    halo_in,
    weights,
    near_taps,
    near,
    ends_out,
    ends_in,
    starts_out,
    starts_in,
    load_sems,
    sems,
    own_sem,
    block_sems,
):
    me = lax.axis_index("seq")
    blocks = x_hbm.shape[1] // LANES
    parts = n // blocks
    rows = MODES // parts
    following = lax.rem(me + 1, n)
    wanted = x_hbm.shape[1] // PIECES
    row_y = lax.div(me, DEEP * parts)
    row_z = lax.rem(lax.div(me, parts), DEEP)

    def block_at(z, y):
        ahead_y = lax.rem(row_y + far_first(y, WIDE), WIDE)
        ahead_z = lax.rem(row_z + far_first(z, DEEP), DEEP)
        return ahead_y * DEEP + ahead_z

    small = [(rate_hbm, rate), (taps_hbm, taps), (residue_hbm, residue), (skip_hbm, skip)]
    loads = [
        pltpu.make_async_copy(src, dst, load_sems.at[i]) for i, (src, dst) in enumerate(small)
    ]

    def fetch(piece):
        span = pl.ds(pl.multiple_of(piece * wanted, wanted), wanted)
        return pltpu.make_async_copy(
            x_hbm.at[:, span, :], xv.at[:, span, :], load_sems.at[len(small) + piece]
        )

    for load in loads[:2]:
        load.start()
    for piece in range(PIECES):
        fetch(piece).start()
    for load in loads[2:]:
        load.start()

    barrier = pltpu.get_barrier_semaphore()

    def greet(i, carry):
        pl.semaphore_signal(
            barrier, inc=1, device_id={"seq": lax.rem(me + i, n)}, device_id_type=MESH
        )
        return carry

    lax.fori_loop(1, n, greet, 0)

    sub = lax.broadcasted_iota(jnp.int32, (CHUNKS, LANES), 0)
    top = sub == 0
    place = lax.broadcasted_iota(jnp.int32, (LANES, LANES), 0)
    token = lax.broadcasted_iota(jnp.int32, (LANES, LANES), 1)
    spread = jnp.where(
        token == lax.rem(place, CHUNKS) * STEPS + lax.div(place, CHUNKS), 1.0, 0.0
    ).astype(BF16)

    loads[0].wait()

    def prepare(block, carry):
        c = cols(block)
        r = rate[:, c]
        decay[:, c] = jnp.exp(-r)
        decay14[:, c] = jnp.exp(-14.0 * r)
        decay15[:, c] = jnp.exp(-15.0 * r)
        return carry

    lax.fori_loop(0, blocks, prepare, 0)

    loads[1].wait()

    def local(block, carry):
        c = cols(block)
        feats = []
        halo_rows = jnp.zeros((CHUNKS, LANES), F32)
        for stream in range(3):
            moved = lax.dot_general(
                spread,
                xv[stream, c, :],
                (((1,), (1,)), ((), ())),
                preferred_element_type=F32,
            )
            v = [moved[j * CHUNKS : (j + 1) * CHUNKS] for j in range(STEPS)]
            for k in range(2):
                row = 2 * stream + k
                halo_rows = jnp.where(
                    sub == row, pltpu.roll(v[14 + k], row + 1, 0), halo_rows
                )
            back1 = jnp.where(top, 0.0, pltpu.roll(v[15], 1, 0))
            back2 = jnp.where(top, 0.0, pltpu.roll(v[14], 1, 0))
            v = [back2, back1] + v
            f = [wide(taps[k, pl.ds(stream, 1), c]) for k in range(3)]
            feat = [f[0] * v[j + 2] + f[1] * v[j + 1] + f[2] * v[j] for j in range(STEPS)]
            if stream == 0:
                for j in range(STEPS):
                    feat0[j * CHUNKS : (j + 1) * CHUNKS, c] = feat[j]
            else:
                for k in range(2):
                    at = (2 * (stream - 1) + k) * CHUNKS
                    first[at : at + CHUNKS, c] = feat[k]
                feats.append(feat)
        halo_out[:, c] = halo_rows.astype(BF16)
        g = [rounded(feats[0][j] * feats[1][j]) for j in range(STEPS)]
        for j in range(STEPS):
            gated[j * CHUNKS : (j + 1) * CHUNKS, c] = g[j]
        for mode in range(MODES):
            a = wide(decay[pl.ds(mode, 1), c])
            state = g[0]
            for j in range(1, STEPS):
                state = a * state + g[j]
            states[mode * CHUNKS : (mode + 1) * CHUNKS, c] = state
        return carry

    def local_piece(piece, carry):
        fetch(piece).wait()
        first_block = piece * (blocks // PIECES)
        return lax.fori_loop(
            0, blocks // PIECES, lambda i, v: local(first_block + i, v), carry, unroll=LOCAL_UNROLL
        )

    lax.fori_loop(0, PIECES, local_piece, 0)
    for load in loads[2:]:
        load.wait()

    pl.semaphore_wait(barrier, n - 1)
    halo = pltpu.make_async_remote_copy(
        src_ref=halo_out,
        dst_ref=halo_in,
        send_sem=sems.at[0],
        recv_sem=sems.at[1],
        device_id={"seq": following},
        device_id_type=MESH,
    )
    halo.start()

    def tables(block, carry):
        c = cols(block)
        r = rate[:, c]
        a = decay[:, c]
        w = residue[:, c] * jnp.sqrt(one_minus_exp(2.0 * r))
        direct = skip[pl.ds(block, 1), :]
        for j in range(STEPS):
            near_taps[pl.ds(j, 1), c] = jnp.sum(w, axis=0, keepdims=True) + direct
            direct = 0.0
            w = w * a
            weights[j * MODES : (j + 1) * MODES, c] = w
        return carry

    lax.fori_loop(0, blocks, tables, 0)
    halo.wait()

    late = (CHUNKS - 1 - sub).astype(F32) * float(-STEPS)

    def finish(block, carry):
        c = cols(block)
        h = jnp.where(me == 0, 0.0, halo_in[:, c].astype(F32))

        def add_first(stream):
            f1 = taps[1, pl.ds(stream, 1), c]
            f2 = taps[2, pl.ds(stream, 1), c]
            h2 = h[2 * stream : 2 * stream + 1]
            h1 = h[2 * stream + 1 : 2 * stream + 2]
            return [
                jnp.where(top, wide(f1 * h1 + f2 * h2), 0.0),
                jnp.where(top, wide(f2 * h1), 0.0),
            ]

        more = [add_first(stream) for stream in range(3)]
        change = []
        for k in range(2):
            at = slice(k * CHUNKS, (k + 1) * CHUNKS)
            feat0[at, c] = feat0[at, c] + more[0][k]
            one = first[k * CHUNKS : (k + 1) * CHUNKS, c] + more[1][k]
            two = first[(2 + k) * CHUNKS : (3 + k) * CHUNKS, c] + more[2][k]
            g = rounded(one * two)
            change.append(g - gated[at, c])
            gated[at, c] = g
        sums = []
        for mode in range(MODES):
            at = slice(mode * CHUNKS, (mode + 1) * CHUNKS)
            state = (
                states[at, c]
                + wide(decay15[pl.ds(mode, 1), c]) * change[0]
                + wide(decay14[pl.ds(mode, 1), c]) * change[1]
            )
            states[at, c] = state
            sums.append(
                jnp.sum(
                    state * jnp.exp(wide(rate[pl.ds(mode, 1), c]) * late), axis=0, keepdims=True
                )
            )
        for part in range(parts):
            ends_out[block * parts + part] = jnp.concatenate(
                sums[part * rows : (part + 1) * rows], axis=0
            ).astype(BF16)
        return carry

    def send_block(src, dst, send_sem, recv_sem, block):
        for part in range(parts):
            k = block * parts + part

            @pl.when(k != me)
            def _():
                pltpu.make_async_remote_copy(
                    src_ref=src.at[k],
                    dst_ref=dst.at[me],
                    send_sem=sems.at[send_sem],
                    recv_sem=recv_sem,
                    device_id={"seq": k},
                    device_id_type=MESH,
                ).start()

    def others(src, dst, send_sem, recv_sem):
        return pltpu.make_async_remote_copy(
            src_ref=src.at[pl.ds(0, n - 1)],
            dst_ref=dst.at[pl.ds(0, n - 1)],
            send_sem=sems.at[send_sem],
            recv_sem=recv_sem,
            device_id={"seq": following},
            device_id_type=MESH,
        )

    def send_ends(z):
        for y in range(WIDE):
            send_block(ends_out, ends_in, 2, sems.at[3], block_at(z, y))

    def finish_group(z, carry):
        for y in range(WIDE):
            finish(block_at(z, y), 0)

        @pl.when(z > 0)
        def _():
            send_ends(z - 1)

        return carry

    lax.fori_loop(0, DEEP, finish_group, 0)
    send_ends(DEEP - 1)
    own = pltpu.make_async_copy(ends_out.at[me], ends_in.at[me], own_sem.at[0])
    own.start()

    def inside(block, carry):
        c = cols(block)
        g = [gated[j * CHUNKS : (j + 1) * CHUNKS, c] for j in range(STEPS)]
        taps_here = [wide(near_taps[pl.ds(j, 1), c]) for j in range(STEPS)]
        for j in range(STEPS):
            total = taps_here[0] * g[j]
            for i in range(1, j + 1):
                total = total + taps_here[i] * g[j - i]
            near[j * CHUNKS : (j + 1) * CHUNKS, c] = total
        for mode in range(MODES):
            at = slice(mode * CHUNKS, (mode + 1) * CHUNKS)
            step = jnp.exp(wide(rate[pl.ds(mode, 1), c]) * float(-STEPS))
            state = states[at, c]
            for shift in (1, 2, 4):
                state = state + jnp.where(sub < shift, 0.0, step * pltpu.roll(state, shift, 0))
                step = step * step
            states[at, c] = jnp.where(top, 0.0, pltpu.roll(state, 1, 0))
        return carry

    lax.fori_loop(0, blocks, inside, 0)

    mine = lax.div(me, parts)
    part = lax.rem(me, parts)
    r = rate[:, cols(mine)]
    pick = r[0:rows]
    for k in range(1, parts):
        pick = jnp.where(part == k, r[k * rows : (k + 1) * rows], pick)
    across = jnp.exp(pick * float(-LANES))

    own.wait()
    others(ends_out, ends_in, 2, sems.at[3]).wait_recv()

    def carry_on(source, entering):
        starts_out[source] = entering.astype(BF16)
        return across * entering + ends_in[source].astype(F32)

    lax.fori_loop(0, n, carry_on, jnp.zeros((rows, LANES), F32), unroll=8)

    def send_starts(z, carry):
        for y in range(WIDE):
            send_block(starts_out, starts_in, 4, block_sems.at[mine], block_at(z, y))
        return carry

    lax.fori_loop(0, DEEP, send_starts, 0)
    pltpu.make_async_copy(starts_out.at[me], starts_in.at[me], block_sems.at[mine]).start()

    early = sub.astype(F32) * float(-STEPS)

    def final(block, carry):
        c = cols(block)
        entering = []
        for mode in range(MODES):
            at = slice(mode * CHUNKS, (mode + 1) * CHUNKS)
            if mode % rows == 0:
                group = starts_in[block * parts + mode // rows].astype(F32)
            row = mode % rows
            entering.append(
                states[at, c]
                + wide(group[row : row + 1]) * jnp.exp(wide(rate[pl.ds(mode, 1), c]) * early)
            )
        results = []
        for j in range(STEPS):
            total = near[j * CHUNKS : (j + 1) * CHUNKS, c]
            for mode in range(MODES):
                total = total + wide(weights[pl.ds(j * MODES + mode, 1), c]) * entering[mode]
            results.append(feat0[j * CHUNKS : (j + 1) * CHUNKS, c] * rounded(total))
        turned = jnp.concatenate(results, axis=0).T.astype(BF16)
        out[c, :] = jnp.dot(turned, spread, preferred_element_type=F32).astype(BF16)
        return carry

    def put(block):
        return pltpu.make_async_copy(out.at[cols(block), :], out_hbm.at[cols(block), :], own_sem.at[1])

    def put_group(z):
        for y in range(WIDE):
            put(block_at(z, y)).start()

    def final_group(i, carry):
        z = DEEP - 1 - i
        for y in range(WIDE):
            block = block_at(z, y)
            slots = pl.ds(block * parts, parts)
            pltpu.make_async_copy(
                starts_out.at[slots], starts_in.at[slots], block_sems.at[block]
            ).wait()
        for y in range(WIDE):
            final(block_at(z, y), 0)

        @pl.when(i > 0)
        def _():
            put_group(z + 1)

        return carry

    lax.fori_loop(0, DEEP, final_group, 0)
    put_group(0)
    others(ends_out, ends_in, 2, sems.at[3]).wait_send()
    others(starts_out, starts_in, 4, sems.at[3]).wait_send()
    pltpu.make_async_copy(out, out_hbm, own_sem.at[1]).wait()


def body(n, qkv, short_filter, decay_rate, residue, skip):
    channels, width = qkv.shape[1:]
    blocks = channels // LANES
    parts = n // blocks
    rows = MODES // parts
    anywhere = pl.BlockSpec(memory_space=pl.ANY)
    full = (LANES, channels)
    packet = (n, rows, LANES)
    return pl.pallas_call(
        functools.partial(kernel, n),
        out_shape=jax.ShapeDtypeStruct((channels, width), BF16),
        in_specs=[anywhere] * 5,
        out_specs=anywhere,
        scratch_shapes=[
            pltpu.VMEM((channels, width), BF16),
            pltpu.VMEM(qkv.shape, BF16),
            pltpu.VMEM(short_filter.shape, F32),
            pltpu.VMEM((MODES, channels), F32),
            pltpu.VMEM((MODES, channels), F32),
            pltpu.VMEM((blocks, LANES), F32),
            pltpu.VMEM((MODES, channels), F32),
            pltpu.VMEM((MODES, channels), F32),
            pltpu.VMEM((MODES, channels), F32),
            pltpu.VMEM(full, F32),
            pltpu.VMEM(full, F32),
            pltpu.VMEM((4 * CHUNKS, channels), F32),
            pltpu.VMEM(full, F32),
            pltpu.VMEM((CHUNKS, channels), BF16),
            pltpu.VMEM((CHUNKS, channels), BF16),
            pltpu.VMEM((STEPS * MODES, channels), F32),
            pltpu.VMEM((STEPS, channels), F32),
            pltpu.VMEM(full, F32),
            pltpu.VMEM(packet, BF16),
            pltpu.VMEM(packet, BF16),
            pltpu.VMEM(packet, BF16),
            pltpu.VMEM(packet, BF16),
            pltpu.SemaphoreType.DMA((4 + PIECES,)),
            pltpu.SemaphoreType.DMA((5,)),
            pltpu.SemaphoreType.DMA((2,)),
            pltpu.SemaphoreType.DMA((blocks,)),
        ],
        compiler_params=pltpu.CompilerParams(collective_id=0, has_side_effects=True),
        name="modal_convolution",
    )(qkv, short_filter, decay_rate.T, residue.T, skip.reshape(blocks, LANES))


def solution(mesh):
    in_specs = (P(None, "ch", "seq"), P(None, None, "ch"), P("ch", None), P("ch", None), P("ch"))
    out_specs = P("ch", "seq")
    return jax.shard_map(
        functools.partial(body, mesh.shape["seq"]),
        mesh=mesh,
        in_specs=in_specs,
        out_specs=out_specs,
        check_vma=False,
    )
```

```python
import functools

import jax
import jax.numpy as jnp
from jax import lax
from jax.experimental import pallas as pl
from jax.experimental.pallas import tpu as pltpu
from jax.sharding import PartitionSpec as P

MODES = 16
SHORT = 3
MESH = pl.DeviceIdType.MESH
LANES = 128
CHUNKS = 8
STEPS = 16
WIDE = 4
DEEP = 8
PIECES = 4
LOCAL_UNROLL = 2
TURN_UNROLL = 4
BEFORE = 8
F32 = jnp.float32
BF16 = jnp.bfloat16


def cols(block):
    return pl.ds(pl.multiple_of(block * LANES, LANES), LANES)


def far_first(i, size):
    half = lax.div(i + 1, 2)
    return lax.rem(size + size // 2 + jnp.where(lax.rem(i, 2) == 1, half, -half), size)


def wide(row):
    return jnp.broadcast_to(row, (CHUNKS, LANES))


def rounded(value):
    return value.astype(BF16).astype(F32)


def one_minus_exp(x):
    series = 1.0 - x * (1.0 / 7.0)
    for k in (6, 5, 4, 3, 2):
        series = 1.0 - x * (1.0 / k) * series
    return jnp.where(x < 0.25, x * series, 1.0 - jnp.exp(-x))


def kernel(
    n,
    x_hbm,
    taps_hbm,
    rate_hbm,
    residue_hbm,
    skip_hbm,
    out_hbm,
    out,
    xv,
    taps,
    rate,
    residue,
    skip,
    decay,
    decay14,
    decay15,
    gated,
    states,
    first,
    feat0,
    turned,
    entry_scale,
    halo_out,
    halo_in,
    halo0_out,
    halo0_in,
    weights,
    near_taps,
    near,
    ends_out,
    ends_in,
    starts_out,
    starts_in,
    load_sems,
    sems,
    own_sem,
    block_sems,
):
    me = lax.axis_index("seq")
    blocks = x_hbm.shape[1] // LANES
    parts = n // blocks
    rows = MODES // parts
    following = lax.rem(me + 1, n)
    wanted = x_hbm.shape[1] // PIECES
    row_y = lax.div(me, DEEP * parts)
    row_z = lax.rem(lax.div(me, parts), DEEP)

    def block_at(z, y):
        ahead_y = lax.rem(row_y + far_first(y, WIDE), WIDE)
        ahead_z = lax.rem(row_z + far_first(z, DEEP), DEEP)
        return ahead_y * DEEP + ahead_z

    small = [(rate_hbm, rate), (taps_hbm, taps), (residue_hbm, residue), (skip_hbm, skip)]
    loads = [
        pltpu.make_async_copy(src, dst, load_sems.at[i]) for i, (src, dst) in enumerate(small)
    ]

    def fetch(piece):
        span = pl.ds(pl.multiple_of(piece * wanted, wanted), wanted)
        return pltpu.make_async_copy(
            x_hbm.at[pl.ds(1, 2), span, :],
            xv.at[pl.ds(1, 2), span, :],
            load_sems.at[len(small) + 1 + piece],
        )

    loads.append(pltpu.make_async_copy(x_hbm.at[0], xv.at[0], load_sems.at[len(small)]))
    for load in loads[:2]:
        load.start()
    for piece in range(PIECES):
        fetch(piece).start()
    for load in loads[2:]:
        load.start()

    barrier = pltpu.get_barrier_semaphore()

    def everyone_else(visit):
        def row(z, carry):
            for y in range(WIDE):
                for part in range(parts):
                    visit(block_at(z, y) * parts + part)
            return carry

        lax.fori_loop(0, DEEP - 1, row, 0)
        near_by(visit)

    def near_by(visit):
        for y in range(WIDE - 1):
            for part in range(parts):
                visit(block_at(DEEP - 1, y) * parts + part)
        for part in range(1, parts):
            visit(me - lax.rem(me, parts) + lax.rem(me + part, parts))

    def greet(k):
        pl.semaphore_signal(barrier, inc=1, device_id={"seq": k}, device_id_type=MESH)

    everyone_else(greet)

    sub = lax.broadcasted_iota(jnp.int32, (CHUNKS, LANES), 0)
    top = sub == 0
    place = lax.broadcasted_iota(jnp.int32, (LANES, LANES), 0)
    token = lax.broadcasted_iota(jnp.int32, (LANES, LANES), 1)
    spread = jnp.where(
        token == lax.rem(place, CHUNKS) * STEPS + lax.div(place, CHUNKS), 1.0, 0.0
    ).astype(BF16)

    def turn(stream, c):
        moved = lax.dot_general(
            spread, xv[stream, c, :], (((1,), (1,)), ((), ())), preferred_element_type=F32
        )
        return [moved[j * CHUNKS : (j + 1) * CHUNKS] for j in range(STEPS)]

    def tails(streams):
        rows_of = jnp.zeros((CHUNKS, LANES), F32)
        for i, v in enumerate(streams):
            for k in range(2):
                row = 2 * i + k
                rows_of = jnp.where(sub == row, pltpu.roll(v[14 + k], row + 1, 0), rows_of)
        return rows_of[0:4].astype(BF16)

    def filtered(stream, c, v):
        back1 = jnp.where(top, 0.0, pltpu.roll(v[15], 1, 0))
        back2 = jnp.where(top, 0.0, pltpu.roll(v[14], 1, 0))
        v = [back2, back1] + v
        f = [wide(taps[k, pl.ds(stream, 1), c]) for k in range(3)]
        return [f[0] * v[j + 2] + f[1] * v[j + 1] + f[2] * v[j] for j in range(STEPS)]

    def from_before(stream, c, h):
        f1 = taps[1, pl.ds(stream, 1), c]
        f2 = taps[2, pl.ds(stream, 1), c]
        return [
            jnp.where(top, wide(f1 * h[1:2] + f2 * h[0:1]), 0.0),
            jnp.where(top, wide(f2 * h[1:2]), 0.0),
        ]

    def spread_out(pair, carry):
        both = pl.ds(pl.multiple_of(pair * 2 * LANES, 2 * LANES), 2 * LANES)
        moved = []
        for i in range(2):
            moved.append(
                lax.dot_general(
                    spread,
                    xv[i + 1, both, :],
                    (((1,), (1,)), ((), ())),
                    preferred_element_type=F32,
                )
            )
            turned[i * LANES : (i + 1) * LANES, both] = moved[i]
        for half in range(2):
            halo_out[:, cols(2 * pair + half)] = tails(
                [
                    [
                        moved[i][
                            j * CHUNKS : (j + 1) * CHUNKS, half * LANES : (half + 1) * LANES
                        ]
                        for j in range(STEPS)
                    ]
                    for i in range(2)
                ]
            )
        return carry

    def spread_piece(piece, carry):
        fetch(piece).wait()
        pairs = blocks // PIECES // 2
        return lax.fori_loop(
            0,
            pairs,
            lambda i, v: spread_out(piece * pairs + i, v),
            carry,
            unroll=TURN_UNROLL,
        )

    lax.fori_loop(0, PIECES, spread_piece, 0)

    loads[0].wait()
    loads[1].wait()

    def prepare(block, carry):
        c = cols(block)
        decay[:, c] = jnp.exp(-rate[:, c])
        return carry

    lax.fori_loop(0, blocks, prepare, 0, unroll=4)

    def local(block, carry):
        c = cols(block)
        feats = []
        for i in range(2):
            v = [
                turned[i * LANES + j * CHUNKS : i * LANES + (j + 1) * CHUNKS, c]
                for j in range(STEPS)
            ]
            feat = filtered(i + 1, c, v)
            for k in range(2):
                at = (2 * i + k) * CHUNKS
                first[at : at + CHUNKS, c] = feat[k]
            feats.append(feat)
        g = [rounded(feats[0][j] * feats[1][j]) for j in range(STEPS)]
        for j in range(STEPS):
            gated[j * CHUNKS : (j + 1) * CHUNKS, c] = g[j]
        for mode in range(MODES):
            a = wide(decay[pl.ds(mode, 1), c])
            state = g[0]
            for j in range(1, STEPS):
                state = a * state + g[j]
            states[mode * CHUNKS : (mode + 1) * CHUNKS, c] = state
        return carry

    lax.fori_loop(0, BEFORE, local, 0, unroll=LOCAL_UNROLL)

    pl.semaphore_wait(barrier, n - 1)

    def to_following(src, dst, sem):
        return pltpu.make_async_remote_copy(
            src_ref=src,
            dst_ref=dst,
            send_sem=sems.at[sem],
            recv_sem=sems.at[sem + 1],
            device_id={"seq": following},
            device_id_type=MESH,
        )

    halo = to_following(halo_out, halo_in, 0)
    halo.start()
    lax.fori_loop(BEFORE, blocks, local, 0, unroll=LOCAL_UNROLL)

    def powers(block, carry):
        c = cols(block)
        a = decay[:, c]
        a2 = a * a
        a4 = a2 * a2
        a14 = a4 * a4 * a4 * a2
        decay14[:, c] = a14
        decay15[:, c] = a14 * a
        return carry

    lax.fori_loop(0, blocks, powers, 0, unroll=4)
    halo.wait()

    late = (CHUNKS - 1 - sub).astype(F32) * float(-STEPS)

    def finish(block, carry):
        c = cols(block)
        h = jnp.where(me == 0, 0.0, halo_in[:, c].astype(F32))

        more = [from_before(i + 1, c, h[2 * i : 2 * i + 2]) for i in range(2)]
        change = []
        for k in range(2):
            at = slice(k * CHUNKS, (k + 1) * CHUNKS)
            one = first[k * CHUNKS : (k + 1) * CHUNKS, c] + more[0][k]
            two = first[(2 + k) * CHUNKS : (3 + k) * CHUNKS, c] + more[1][k]
            g = rounded(one * two)
            change.append(g - gated[at, c])
            gated[at, c] = g
        sums = []
        for mode in range(MODES):
            at = slice(mode * CHUNKS, (mode + 1) * CHUNKS)
            state = (
                states[at, c]
                + wide(decay15[pl.ds(mode, 1), c]) * change[0]
                + wide(decay14[pl.ds(mode, 1), c]) * change[1]
            )
            states[at, c] = state
            sums.append(
                jnp.sum(
                    state * jnp.exp(wide(rate[pl.ds(mode, 1), c]) * late), axis=0, keepdims=True
                )
            )
        for part in range(parts):
            ends_out[block * parts + part] = jnp.concatenate(
                sums[part * rows : (part + 1) * rows], axis=0
            ).astype(BF16)
        return carry

    def sender(src, dst, send_sem, recv_sem):
        def send(k):
            pltpu.make_async_remote_copy(
                src_ref=src.at[k],
                dst_ref=dst.at[me],
                send_sem=sems.at[send_sem],
                recv_sem=recv_sem,
                device_id={"seq": k},
                device_id_type=MESH,
            ).start()

        return send

    def others(src, dst, send_sem, recv_sem):
        return pltpu.make_async_remote_copy(
            src_ref=src.at[pl.ds(0, n - 1)],
            dst_ref=dst.at[pl.ds(0, n - 1)],
            send_sem=sems.at[send_sem],
            recv_sem=recv_sem,
            device_id={"seq": following},
            device_id_type=MESH,
        )

    send_end = sender(ends_out, ends_in, 2, sems.at[3])

    def finish_group(z, carry):
        for y in range(WIDE):
            finish(block_at(z, y), 0)

        @pl.when(z > 0)
        def _():
            for y in range(WIDE):
                for part in range(parts):
                    send_end(block_at(z - 1, y) * parts + part)

        return carry

    lax.fori_loop(0, DEEP, finish_group, 0)
    near_by(send_end)
    own = pltpu.make_async_copy(ends_out.at[me], ends_in.at[me], own_sem.at[0])
    own.start()

    loads[4].wait()

    def query(block, carry):
        c = cols(block)
        v = turn(0, c)
        halo0_out[:, c] = tails([v])
        feat = filtered(0, c, v)
        for j in range(STEPS):
            feat0[j * CHUNKS : (j + 1) * CHUNKS, c] = feat[j]
        return carry

    lax.fori_loop(0, blocks, query, 0, unroll=2)
    halo0 = to_following(halo0_out, halo0_in, 5)
    halo0.start()
    loads[2].wait()
    loads[3].wait()

    def tables(block, carry):
        c = cols(block)
        r = rate[:, c]
        a = decay[:, c]
        w = residue[:, c] * jnp.sqrt(one_minus_exp(2.0 * r))
        direct = skip[pl.ds(block, 1), :]
        for j in range(STEPS):
            near_taps[pl.ds(j, 1), c] = jnp.sum(w, axis=0, keepdims=True) + direct
            direct = 0.0
            w = w * a
            if j == 0:
                weights[:, c] = w
        return carry

    lax.fori_loop(0, blocks, tables, 0)

    early = sub.astype(F32) * float(-STEPS)

    def inside(block, carry):
        c = cols(block)
        g = [gated[j * CHUNKS : (j + 1) * CHUNKS, c] for j in range(STEPS)]
        taps_here = [wide(near_taps[pl.ds(j, 1), c]) for j in range(STEPS)]
        for j in range(STEPS):
            total = taps_here[0] * g[j]
            for i in range(1, j + 1):
                total = total + taps_here[i] * g[j - i]
            near[j * CHUNKS : (j + 1) * CHUNKS, c] = total
        for mode in range(MODES):
            at = slice(mode * CHUNKS, (mode + 1) * CHUNKS)
            step = jnp.exp(wide(rate[pl.ds(mode, 1), c]) * float(-STEPS))
            state = states[at, c]
            for shift in (1, 2, 4):
                state = state + jnp.where(sub < shift, 0.0, step * pltpu.roll(state, shift, 0))
                step = step * step
            w = wide(weights[pl.ds(mode, 1), c])
            states[at, c] = jnp.where(top, 0.0, w * pltpu.roll(state, 1, 0))
            entry_scale[at, c] = w * jnp.exp(wide(rate[pl.ds(mode, 1), c]) * early)
        return carry

    lax.fori_loop(0, blocks, inside, 0)

    mine = lax.div(me, parts)
    part = lax.rem(me, parts)
    r = rate[:, cols(mine)]
    pick = r[0:rows]
    for k in range(1, parts):
        pick = jnp.where(part == k, r[k * rows : (k + 1) * rows], pick)
    across = jnp.exp(pick * float(-LANES))

    own.wait()
    others(ends_out, ends_in, 2, sems.at[3]).wait_recv()

    def carry_on(source, entering):
        starts_out[source] = entering.astype(BF16)
        return across * entering + ends_in[source].astype(F32)

    lax.fori_loop(0, n, carry_on, jnp.zeros((rows, LANES), F32), unroll=8)

    everyone_else(sender(starts_out, starts_in, 4, block_sems.at[mine]))
    pltpu.make_async_copy(starts_out.at[me], starts_in.at[me], block_sems.at[mine]).start()

    halo0.wait()

    def final(block, carry):
        c = cols(block)
        entering = []
        for mode in range(MODES):
            at = slice(mode * CHUNKS, (mode + 1) * CHUNKS)
            if mode % rows == 0:
                group = starts_in[block * parts + mode // rows].astype(F32)
            row = mode % rows
            entering.append(
                states[at, c] + wide(group[row : row + 1]) * entry_scale[at, c]
            )
        before = from_before(0, c, jnp.where(me == 0, 0.0, halo0_in[:, c].astype(F32)))
        falls = [wide(decay[pl.ds(mode, 1), c]) for mode in range(MODES)]
        results = []
        for j in range(STEPS):
            total = near[j * CHUNKS : (j + 1) * CHUNKS, c]
            for mode in range(MODES):
                total = total + entering[mode]
            if j < STEPS - 1:
                entering = [entering[mode] * falls[mode] for mode in range(MODES)]
            query_here = feat0[j * CHUNKS : (j + 1) * CHUNKS, c]
            if j < 2:
                query_here = query_here + before[j]
            results.append(query_here * rounded(total))
        whole = jnp.concatenate(results, axis=0).T.astype(BF16)
        out[c, :] = jnp.dot(whole, spread, preferred_element_type=F32).astype(BF16)
        return carry

    def put(block):
        return pltpu.make_async_copy(out.at[cols(block), :], out_hbm.at[cols(block), :], own_sem.at[1])

    def put_group(z):
        for y in range(WIDE):
            put(block_at(z, y)).start()

    def final_group(i, carry):
        z = DEEP - 1 - i
        for y in range(WIDE):
            block = block_at(z, y)
            slots = pl.ds(block * parts, parts)
            pltpu.make_async_copy(
                starts_out.at[slots], starts_in.at[slots], block_sems.at[block]
            ).wait()
        for y in range(WIDE):
            final(block_at(z, y), 0)

        @pl.when(i > 0)
        def _():
            put_group(z + 1)

        return carry

    lax.fori_loop(0, DEEP, final_group, 0)
    put_group(0)
    others(ends_out, ends_in, 2, sems.at[3]).wait_send()
    others(starts_out, starts_in, 4, sems.at[3]).wait_send()
    pltpu.make_async_copy(out, out_hbm, own_sem.at[1]).wait()


def body(n, qkv, short_filter, decay_rate, residue, skip):
    channels, width = qkv.shape[1:]
    blocks = channels // LANES
    parts = n // blocks
    rows = MODES // parts
    anywhere = pl.BlockSpec(memory_space=pl.ANY)
    full = (LANES, channels)
    packet = (n, rows, LANES)
    result = pl.pallas_call(
        functools.partial(kernel, n),
        out_shape=jax.ShapeDtypeStruct((channels, width), BF16),
        in_specs=[anywhere] * 5,
        out_specs=anywhere,
        scratch_shapes=[
            pltpu.VMEM((channels, width), BF16),
            pltpu.VMEM(qkv.shape, BF16),
            pltpu.VMEM(short_filter.shape, F32),
            pltpu.VMEM((MODES, channels), F32),
            pltpu.VMEM((MODES, channels), F32),
            pltpu.VMEM((blocks, LANES), F32),
            pltpu.VMEM((MODES, channels), F32),
            pltpu.VMEM((MODES, channels), F32),
            pltpu.VMEM((MODES, channels), F32),
            pltpu.VMEM(full, F32),
            pltpu.VMEM(full, F32),
            pltpu.VMEM((4 * CHUNKS, channels), F32),
            pltpu.VMEM(full, F32),
            pltpu.VMEM((2 * LANES, channels), F32),
            pltpu.VMEM(full, F32),
            pltpu.VMEM((4, channels), BF16),
            pltpu.VMEM((4, channels), BF16),
            pltpu.VMEM((4, channels), BF16),
            pltpu.VMEM((4, channels), BF16),
            pltpu.VMEM((MODES, channels), F32),
            pltpu.VMEM((STEPS, channels), F32),
            pltpu.VMEM(full, F32),
            pltpu.VMEM(packet, BF16),
            pltpu.VMEM(packet, BF16),
            pltpu.VMEM(packet, BF16),
            pltpu.VMEM(packet, BF16),
            pltpu.SemaphoreType.DMA((5 + PIECES,)),
            pltpu.SemaphoreType.DMA((7,)),
            pltpu.SemaphoreType.DMA((2,)),
            pltpu.SemaphoreType.DMA((blocks,)),
        ],
        compiler_params=pltpu.CompilerParams(collective_id=0, has_side_effects=True),
        name="modal_convolution",
    )(qkv, short_filter, decay_rate.T, residue.T, skip.reshape(blocks, LANES))
    return settled(result)


def hand_over(src, dst, held, sems):
    rows = src.shape[0] // PIECES
    moves = []
    for piece in range(PIECES):
        span = pl.ds(piece * rows, rows)
        moves.append(
            (
                pltpu.make_async_copy(src.at[span, :], held.at[span, :], sems.at[0, piece]),
                pltpu.make_async_copy(held.at[span, :], dst.at[span, :], sems.at[1, piece]),
            )
        )
    for into, _ in moves:
        into.start()
    for into, out in moves:
        into.wait()
        out.start()
    for _, out in moves:
        out.wait()


def settled(array):
    anywhere = pl.BlockSpec(memory_space=pl.ANY)
    return pl.pallas_call(
        hand_over,
        out_shape=jax.ShapeDtypeStruct(array.shape, array.dtype),
        in_specs=[anywhere],
        out_specs=anywhere,
        scratch_shapes=[
            pltpu.VMEM(array.shape, array.dtype),
            pltpu.SemaphoreType.DMA((2, PIECES)),
        ],
        name="hand_over",
    )(array)


def solution(mesh):
    in_specs = (P(None, "ch", "seq"), P(None, None, "ch"), P("ch", None), P("ch", None), P("ch"))
    out_specs = P("ch", "seq")
    return jax.shard_map(
        functools.partial(body, mesh.shape["seq"]),
        mesh=mesh,
        in_specs=in_specs,
        out_specs=out_specs,
        check_vma=False,
    )
```
